32 devices in a mesh: ctx: 16 (over z, x, core), ch: 2 (over y).
Axes of the slice: x: 2, y: 2, z: 4, core: 2. Of those that a mesh axis runs over, the one named last changes fastest.
Arguments:
- query_gate: bfloat16 [8192, 1024], P('ctx', 'ch'), may hold values from -6 to 6
- key_gate: bfloat16 [8192, 1024], P('ctx', 'ch'), may hold values from -6 to 6
- value_input: bfloat16 [8192, 1024], P('ctx', 'ch'), may hold values from -6 to 6
- grad_out: bfloat16 [8192, 1024], P('ctx', 'ch'), may hold values from -6 to 6
- filters: float32 [8192, 64], P('ctx'), may hold values from -6 to 6
Outputs:
- layer_out: bfloat16 [8192, 1024], P('ctx', 'ch')
- grad_query: bfloat16 [8192, 1024], P('ctx', 'ch')
- grad_key: bfloat16 [8192, 1024], P('ctx', 'ch')
- grad_value: bfloat16 [8192, 1024], P('ctx', 'ch')
- grad_filters: float32 [8192, 64], P('ctx', 'ch')
The draws below stay inside these ranges and needn't reach their ends.
All inputs are finite; a program needn't handle non-finite values.
Results may differ from the reference program's by a relative error of at most 0.0051.
Values may be sent and summed in bfloat16 or wider, within the bound.
A program may use at most 128 MiB of HBM per device.

```python
import math
import jax
import jax.numpy as jnp
from jax import lax

CH = 1024
FG = 64
SEQ = 8192


def block_levels(rng, extent, cuts, low, top_value):
    level = 1.0
    for position, parts in cuts:
        heights = jax.random.uniform(jax.random.fold_in(jax.random.fold_in(rng, 6), position), (parts,), jnp.float32, low / len(cuts), top_value / len(cuts))
        level = level * jnp.repeat(jnp.exp(heights), extent[position] // parts).reshape((-1,) + (1,) * (len(extent) - 1 - position))
    return level


def noise(stream_key, extent, spread, limit, shards=(), held_as=jnp.bfloat16):
    factor_of = block_levels(stream_key, extent, shards, -0.22, 0.18) if shards else 1.0
    drawn = jax.random.normal(stream_key, extent, jnp.float32) * spread * factor_of
    return jnp.minimum(jnp.maximum(drawn, -limit), limit).astype(held_as)


def setup_inputs(seed: int = 0) -> dict:
    seeds = jax.random.split(jax.random.key(seed), 6)
    return {
        "query_gate": noise(seeds[0], (SEQ, CH), 1.0, 6.0, ((0, 16), (1, 2))),
        "key_gate": noise(seeds[1], (SEQ, CH), 1.0, 6.0, ((0, 16), (1, 2))),
        "value_input": noise(seeds[2], (SEQ, CH), 1.0, 6.0, ((0, 16), (1, 2))),
        "grad_out": noise(seeds[3], (SEQ, CH), 1.0, 6.0, ((0, 16), (1, 2))),
        "filters": noise(seeds[4], (SEQ, FG), 1.0, 6.0, ((0, 16),), jnp.float32),
    }


def reference(query_gate, key_gate, value_input, grad_out, filters):
    seq_length = query_gate.shape[0]
    channels = query_gate.shape[1]
    groups = filters.shape[1]
    fft_length = 2 * seq_length
    filter_scale = 1.0 / math.sqrt(seq_length)
    filter_spec = jnp.fft.rfft(filters * filter_scale, n=fft_length, axis=0)

    def one_block(carry, block_index):

        def take(source):
            return lax.dynamic_slice_in_dim(source, block_index * groups, groups, 1).astype(jnp.float32)
        query_part = take(query_gate)
        key_part = take(key_gate)
        value_part = take(value_input)
        grad_part = take(grad_out)
        signal = lax.optimization_barrier((key_part * value_part).astype(jnp.bfloat16)).astype(jnp.float32)
        grad_signal = lax.optimization_barrier((grad_part * query_part).astype(jnp.bfloat16)).astype(jnp.float32)
        signal_spec = jnp.fft.rfft(signal, n=fft_length, axis=0)
        grad_spec = jnp.fft.rfft(grad_signal, n=fft_length, axis=0)
        mixed = jnp.fft.irfft(filter_spec * signal_spec, n=fft_length, axis=0)[:seq_length]
        back = jnp.fft.irfft(jnp.conj(filter_spec) * grad_spec, n=fft_length, axis=0)[:seq_length]
        layer_part = (query_part * mixed).astype(jnp.bfloat16)
        query_grad = (grad_part * mixed).astype(jnp.bfloat16)
        key_grad = (back * value_part).astype(jnp.bfloat16)
        value_grad = (back * key_part).astype(jnp.bfloat16)
        carry = carry + jnp.conj(signal_spec) * grad_spec
        return (carry, (layer_part, query_grad, key_grad, value_grad))
    blocks = jnp.arange(channels // groups, dtype=jnp.int32)
    summed, pieces = lax.scan(one_block, jnp.zeros_like(filter_spec), blocks)

    def stitch(stacked):
        return jnp.transpose(stacked, (1, 0, 2)).reshape(seq_length, channels)
    grad_filters = jnp.fft.irfft(summed, n=fft_length, axis=0)[:seq_length] * filter_scale
    return (stitch(pieces[0]), stitch(pieces[1]), stitch(pieces[2]), stitch(pieces[3]), grad_filters)
```

```python
import math

import jax
import jax.numpy as jnp
from jax import lax
from jax.experimental import pallas as pl
from jax.experimental.pallas import tpu as pltpu
from jax.sharding import PartitionSpec as P

F32 = jnp.float32
BF16 = jnp.bfloat16
BATCH = 4
LANES = 128


def dot(a, b):
    return lax.dot_general(a, b, (((1,), (0,)), ((), ())), preferred_element_type=F32)


def dot_nt(a, b):
    return lax.dot_general(a, b, (((1,), (1,)), ((), ())), preferred_element_type=F32)


def flip_matrix(size):
    row = lax.broadcasted_iota(jnp.int32, (size, size), 0)
    col = lax.broadcasted_iota(jnp.int32, (size, size), 1)
    return jnp.where(row + col == size - 1, 1.0, 0.0).astype(BF16)


class Plan:
    def __init__(self, n, seq_rows, channels, groups):
        self.n = n
        self.seq_rows = seq_rows
        self.channels = channels
        self.groups = groups
        self.own = groups // n
        self.repeats = channels // groups
        self.padded = max(8, self.repeats)
        if self.own * self.padded < 16:
            self.padded = 16
        self.block = seq_rows // 2
        self.step_rows = 2 * self.padded
        self.rows = n * self.step_rows
        self.blocks = 2 * n
        self.tiles = self.blocks * self.block // LANES
        self.scale = 1.0 / math.sqrt(n * seq_rows)


def build_toeplitz(plan, q, h_ref, toep):
    row = lax.broadcasted_iota(jnp.int32, (LANES, LANES), 0)
    col = lax.broadcasted_iota(jnp.int32, (LANES, LANES), 1)
    keep = col >= row
    toep[q, :, 0:LANES] = jnp.zeros((LANES, LANES), BF16)

    def step(u, before):
        base = pl.multiple_of(u * 8, 8)
        taps = h_ref[q, pl.ds(base, 8), :]
        for k in range(8):
            wide = jnp.broadcast_to(taps[k : k + 1, :], (LANES, LANES))
            now = pltpu.roll(wide, 0, 1, stride=1, stride_axis=0)
            at = pl.multiple_of((base + k + 1) * LANES, LANES)
            toep[q, :, pl.ds(at, LANES)] = jnp.where(keep, now, before).astype(BF16)
            before = now
        return before

    lax.fori_loop(0, plan.tiles // 8, step, jnp.zeros((LANES, LANES), F32))


def arrange(plan, ref, even, odd, down):
    rp = plan.padded
    half = plan.block
    first = plan.rows if down else 0
    last = plan.n - 1

    def step(i, carry):
        wide = ref[i].astype(F32)
        if down:
            other = ref[jnp.maximum(i - 1, 0)].astype(F32)
            other = jnp.where(i > 0, other, 0.0)
        else:
            other = ref[jnp.minimum(i + 1, last)].astype(F32)
            other = jnp.where(i < last, other, 0.0)
        at = pl.multiple_of(first + i * plan.step_rows, 16)
        for q in range(plan.own):
            mine = wide[q * rp : (q + 1) * rp]
            near = other[q * rp : (q + 1) * rp]
            even[q, pl.ds(at, 2 * rp), :] = jnp.concatenate(
                [mine[:, :half], mine[:, half:]], axis=0
            ).astype(BF16)
            pair = [near[:, half:], mine[:, :half]] if down else [mine[:, half:], near[:, :half]]
            odd[q, pl.ds(at, 2 * rp), :] = jnp.concatenate(pair, axis=0).astype(BF16)
        return carry

    lax.fori_loop(0, plan.n, step, 0)
    blank = jnp.zeros((plan.own, plan.rows, half), BF16)
    empty = 0 if down else plan.rows
    even[:, empty : empty + plan.rows, :] = blank
    odd[:, empty : empty + plan.rows, :] = blank


def toeplitz_stack(plan, q, e_block, toep):
    width = plan.block
    parts = []
    for k in range(BATCH):
        at = (e_block * BATCH + k) * width
        if not isinstance(at, int):
            at = pl.multiple_of(at, LANES)
        parts.append(toep[q, :, pl.ds(at + LANES, width)])
        parts.append(toep[q, :, pl.ds(at, width)])
    return jnp.concatenate(parts, axis=0)


def rows_of(start, size):
    if isinstance(start, int):
        return pl.ds(start, size)
    return pl.ds(pl.multiple_of(start, 16), size)


def batches(plan, body):
    count = plan.blocks // BATCH
    if plan.blocks <= 32:
        for e_block in range(count):
            body(e_block, e_block * (BATCH // 2) * plan.step_rows)
    else:

        def step(e_block, carry):
            body(e_block, 0)
            return carry

        lax.fori_loop(0, count, step, 0)


def convolve(plan, q, xs, gs, toep, acc_y, acc_z):
    rows, sr = plan.rows, plan.step_rows

    def body(e_block, skip):
        weights = toeplitz_stack(plan, q, e_block, toep)
        size = rows - skip
        left_x, left_g = [], []
        for k in range(BATCH // 2):
            e = e_block * (BATCH // 2) + k
            for part in range(2):
                left_x.append(xs[part][q, rows_of(rows - e * sr + skip, size), :])
                left_g.append(gs[part][q, rows_of(e * sr, size), :])
        out_y = dot(jnp.concatenate(left_x, axis=1), weights)
        out_z = dot(jnp.concatenate(left_g, axis=1), weights)
        if isinstance(e_block, int) and e_block == 0:
            acc_y[...] = out_y
            acc_z[...] = out_z
        else:
            acc_y[skip:, :] += out_y
            acc_z[:size, :] += out_z

    if plan.blocks > 32:
        acc_y[...] = jnp.zeros_like(acc_y)
        acc_z[...] = jnp.zeros_like(acc_z)
    batches(plan, body)


def correlate(plan, q, xt, gn, kept, sum_a, sum_b):
    rows, sr = plan.rows, plan.step_rows
    row = lax.broadcasted_iota(jnp.int32, (LANES, LANES), 0)
    col = lax.broadcasted_iota(jnp.int32, (LANES, LANES), 1)
    inside = col <= row
    per = BATCH * plan.block // LANES

    def fold(tile, at):
        turned = pltpu.roll(tile, 1, 1, stride=1, stride_axis=0)
        whole = jnp.sum(turned, axis=0, keepdims=True)
        part = jnp.sum(jnp.where(inside, turned, 0.0), axis=0, keepdims=True)
        sum_a[pl.ds(at, 1), :] = part
        sum_b[pl.ds(at, 1), :] = whole - part

    kept[...] = jnp.zeros_like(kept)

    def body(e_block, skip):
        right = []
        for k in range(BATCH // 2):
            e = e_block * (BATCH // 2) + k
            for part in range(2):
                right.append(gn[part][q, rows_of(e * sr, rows), :])
        wide = dot(xt[q], jnp.concatenate(right, axis=1))
        for k in range(per):
            low = wide[0:LANES, k * LANES : (k + 1) * LANES]
            if k == 0:
                high = kept[...]
            else:
                high = wide[LANES:, (k - 1) * LANES : k * LANES]
            fold(low + high, e_block * per + k)
        kept[...] = wide[LANES:, (per - 1) * LANES :]

    batches(plan, body)
    fold(kept[...], plan.tiles)


def compute_kernel(plan, x_ref, g_ref, h_ref, y_ref, z_ref, c_ref, toep, xe, xo, ge, go, re, ro, xt, acc_y, acc_z, kept, sum_a, sum_b):
    flip = flip_matrix(plan.block)
    arrange(plan, x_ref, xe, xo, True)
    arrange(plan, g_ref, ge, go, False)
    sum_a[...] = jnp.zeros_like(sum_a)
    sum_b[...] = jnp.zeros_like(sum_b)

    def one(q, carry):
        build_toeplitz(plan, q, h_ref, toep)
        rows = plan.rows
        re[q, 0:rows, :] = dot(ge[q, 0:rows, :], flip).astype(BF16)
        ro[q, 0:rows, :] = dot(go[q, 0:rows, :], flip).astype(BF16)
        re[q, rows:, :] = jnp.zeros((rows, plan.block), BF16)
        ro[q, rows:, :] = jnp.zeros((rows, plan.block), BF16)
        xt[q] = dot_nt(flip, xe[q, rows:, :]).astype(BF16)
        convolve(plan, q, (xe, xo), (re, ro), toep, acc_y, acc_z)
        y_ref[q] = acc_y[...].astype(BF16)
        z_ref[q] = dot(acc_z[...].astype(BF16), flip).astype(BF16)
        correlate(plan, q, xt, (ge, go), kept, sum_a, sum_b)
        c_ref[q] = (sum_a[1 : plan.tiles + 1, :] + sum_b[2 : plan.tiles + 2, :]) * plan.scale
        return carry

    lax.fori_loop(0, plan.own, one, 0)


def compute_call(plan, x, g, h):
    own, rows, block = plan.own, plan.rows, plan.block
    field = jax.ShapeDtypeStruct((own, rows, block), BF16)
    pad = pltpu.VMEM((own, 2 * rows, block), BF16)
    return pl.pallas_call(
        lambda *refs: compute_kernel(plan, *refs),
        out_shape=(field, field, jax.ShapeDtypeStruct((own, plan.tiles, LANES), F32)),
        in_specs=[pl.BlockSpec(memory_space=pltpu.VMEM)] * 3,
        out_specs=[pl.BlockSpec(memory_space=pltpu.VMEM)] * 3,
        scratch_shapes=[
            pltpu.VMEM((own, LANES, (plan.tiles + 1) * LANES), BF16),
            pad, pad, pad, pad, pad, pad,
            pltpu.VMEM((own, block, rows), BF16),
            pltpu.VMEM((rows, block), F32),
            pltpu.VMEM((rows, block), F32),
            pltpu.VMEM((LANES, LANES), F32),
            pltpu.VMEM((plan.tiles + 8, LANES), F32),
            pltpu.VMEM((plan.tiles + 8, LANES), F32),
        ],
        compiler_params=pltpu.CompilerParams(vmem_limit_bytes=60 * 1024 * 1024),
        name="toeplitz",
    )(x, g, h)


def pick_matrix(plan):
    slot = lax.broadcasted_iota(jnp.int32, (plan.groups, plan.padded, plan.channels), 0)
    rep = lax.broadcasted_iota(jnp.int32, (plan.groups, plan.padded, plan.channels), 1)
    chan = lax.broadcasted_iota(jnp.int32, (plan.groups, plan.padded, plan.channels), 2)
    return jnp.where(rep * plan.groups + slot == chan, 1.0, 0.0).astype(BF16)


def per_device(query_gate, key_gate, value_input, grad_out, filters):
    seq_rows, channels = query_gate.shape
    groups = filters.shape[1]
    n = lax.axis_size("ctx")
    plan = Plan(n, seq_rows, channels, groups)
    own, rp, block = plan.own, plan.padded, plan.block
    query_wide = query_gate.astype(F32)
    key_wide = key_gate.astype(F32)
    value_wide = value_input.astype(F32)
    grad_wide = grad_out.astype(F32)
    signal = (key_wide * value_wide).astype(BF16)
    grad_signal = (grad_wide * query_wide).astype(BF16)
    pick = pick_matrix(plan)
    flat = pick.reshape(groups * rp, channels)

    def swap(array):
        return lax.all_to_all(array, "ctx", split_axis=0, concat_axis=0, tiled=True)

    def spread(values):
        turned = dot_nt(flat, values).astype(BF16)
        return swap(turned.reshape(n, own * rp, seq_rows))

    taps = swap((filters * plan.scale).T.reshape(n, own, seq_rows))
    taps = taps.transpose(1, 0, 2).reshape(own, plan.tiles, LANES)
    x = spread(signal)
    g = spread(grad_signal)
    y, z, corr = compute_call(plan, x, g, taps)

    def gather(field):
        parts = swap(field.reshape(own, n, 2 * rp, block).transpose(1, 0, 2, 3))
        parts = parts.reshape(groups, 2, rp, block)
        out = jnp.einsum("gjrl,grc->jlc", parts, pick, preferred_element_type=F32)
        return out.reshape(seq_rows, channels)

    mixed = gather(y)
    back = gather(z)
    corr = corr.reshape(own, n, seq_rows).transpose(1, 0, 2)
    corr = swap(corr).reshape(groups, seq_rows)
    grad_filters = lax.psum_scatter(corr, "ch", scatter_dimension=0, tiled=True).T
    layer_out = (query_wide * mixed).astype(BF16)
    grad_query = (grad_wide * mixed).astype(BF16)
    grad_key = (back * value_wide).astype(BF16)
    grad_value = (back * key_wide).astype(BF16)
    return (layer_out, grad_query, grad_key, grad_value, grad_filters)


def solution(mesh):
    wide = P("ctx", "ch")
    return jax.shard_map(
        per_device,
        mesh=mesh,
        in_specs=(wide, wide, wide, wide, P("ctx", None)),
        out_specs=(wide, wide, wide, wide, wide),
        check_vma=False,
    )
```
